512 devices in a mesh: dp: 8 (over z_hi, core), expert: 64 (over y, x, z_lo).
Axes of the slice: x: 4, y: 4, z: 16 (z_hi: 4, z_lo: 4; z = z_hi * 4 + z_lo), core: 2. Of those that a mesh axis runs over, the one named last changes fastest.
Arguments:
- tokens: bfloat16 [8192, 3584], P('expert', 'dp'), may hold values from -6 to 6
- out_grad: bfloat16 [8192, 3584], P('expert', 'dp'), may hold values from -6 to 6
- gate_up_weight: bfloat16 [64, 3584, 2048], P('expert', 'dp'), may hold values from -0.09375 to 0.09375
- down_weight: bfloat16 [64, 1024, 3584], P('expert', None, 'dp'), may hold values from -0.1875 to 0.1875
- routes: int32 [8192, 2], P('expert'), may hold values from 0 to 63, all different within a row; in each aligned block of 128 rows (0 to 127, 128 to 255, ...) at most 8 rows name the same one
- route_weight: float32 [8192, 2], P('expert'), may hold values from 0.1 to 1
- swapped: int32 [4], replicated, may hold values from 0 to 31, as said below
Outputs:
- layer_out: bfloat16 [8192, 3584], P('expert', 'dp')
- token_grad: bfloat16 [8192, 3584], P('expert', 'dp')
- down_grad: bfloat16 [64, 1024, 3584], P('expert', None, 'dp')
The draws below stay inside these ranges and needn't reach their ends.
Inputs may be any that keep to these rules, and one draw needn't show every extreme that they name: `routes`: among the rows of each block of 128 consecutive tokens, no expert is named more than 8 times, a bound that some block reaches; a token names different experts. `swapped`: 4 different device numbers; device 0 and device 32 - 1 are always among them.
All inputs are finite; a program needn't handle non-finite values.
Results may differ from the reference program's by a relative error of at most 0.023.
Values may be sent and summed in bfloat16 or wider, within the bound.
A program may use at most 64 MiB of HBM per device.

```python
import math
import jax
import jax.numpy as jnp
import numpy as np
from jax import lax

D = 3584
FF = 1024
TOP = 2
MIGR = 4
TOK_DEV = 128
EXPERTS = 64
PAIRS_ALL = 32
CAP = 8
TOKENS = 8192
N_DP = 8


def draw_swapped(key, part):
    inner = 1 + jax.random.permutation(jax.random.fold_in(key, 11), PAIRS_ALL - 2)[:MIGR - 2]
    listed = jnp.concatenate([jnp.zeros((1,), jnp.int32), inner.astype(jnp.int32), jnp.full((1,), PAIRS_ALL - 1, jnp.int32)])
    order = jax.random.permutation(jax.random.fold_in(key, 12), MIGR)
    return listed[order].astype(jnp.int32)


def steps_of(key, extent, shards, least, high):
    factor_of = 1.0
    for axis_at, blocks in shards:
        steps = jax.random.uniform(jax.random.fold_in(jax.random.fold_in(key, 6), axis_at), (blocks,), jnp.float32, least / len(shards), high / len(shards))
        factor_of = factor_of * jnp.repeat(jnp.exp(steps), extent[axis_at] // blocks).reshape((-1,) + (1,) * (len(extent) - 1 - axis_at))
    return factor_of


def deal_out(key, own, number, rows, count, top, reach, lean):
    ranking = jax.random.permutation(key, count)
    crowded, usual = portions_of(count, rows * top, reach, lean, True), portions_of(count, rows * top, reach, lean, False)
    places = jnp.arange(count)

    def named(tallies, turn):
        used = int((tallies > 0).sum())
        fixed = max(1, used // 4)
        passed = fixed + (places - fixed + turn * (used - fixed)) % max(1, count - fixed)
        return jnp.zeros((count,), jnp.int32).at[ranking[jnp.where(places < fixed, places, passed)]].set(jnp.asarray(tallies, jnp.int32))

    tallies = jnp.where(number % 4 == 0, named(crowded, number // 4), named(usual, number - number // 4 - 1))
    mixed = jax.random.permutation(jax.random.fold_in(own, 3), count)
    source_of, receiver = mixed[0:count // 2 * 2:2], mixed[1:count // 2 * 2:2]
    slack = jnp.minimum(tallies[source_of] - 1, reach - tallies[receiver]) // 2
    slack = jnp.where((source_of == ranking[0]) | (receiver == ranking[0]) | (tallies[receiver] == 0), 0, jnp.maximum(slack, 0))
    passed = jax.random.randint(jax.random.fold_in(own, 4), (count // 2,), 0, 1 << 20) % (slack + 1)
    tallies = tallies.at[source_of].add(-passed).at[receiver].add(passed)
    members = jnp.searchsorted(jnp.cumsum(tallies), jnp.arange(rows * top), side="right").astype(jnp.int32)
    listing = members.reshape(top, rows).T
    listing = listing[jax.random.permutation(jax.random.fold_in(own, 1), rows)]
    turn = jax.random.randint(jax.random.fold_in(own, 2), (rows, 1), 0, top)
    return jnp.take_along_axis(listing, (jnp.arange(top)[None, :] + turn) % top, axis=1)


def portions_of(count, total, limit, lean, full):
    portions = [(1 << 20) // math.isqrt(rank ** lean) + 1 for rank in range(1, count + 1)]
    largest = limit if full else min(limit, max(-(-total // count), total * portions[0] // sum(portions)))
    least = 1 if total - largest >= count - 1 else 0
    counts, rest = [largest] + [least] * (count - 1), total - largest - least * (count - 1)
    while rest > 0:
        movable = [i for i in range(1, count) if counts[i] < largest] or [i for i in range(1, count) if counts[i] < limit]
        whole, remaining = sum([portions[i] for i in movable]), rest
        for i in movable:
            extra = min(limit - counts[i], max(1, remaining * portions[i] // whole), rest)
            counts[i] = counts[i] + extra
            rest = rest - extra
    return np.array(counts)


def bell_draw(key, shape, width, most, split=(), kind=jnp.bfloat16):
    level = steps_of(key, shape, split, -0.22, 0.18) if split else 1.0
    result = jax.random.normal(key, shape, jnp.float32) * width * level
    return jnp.minimum(jnp.maximum(result, -most), most).astype(kind)


def setup_inputs(seed: int = 0) -> dict:
    splits = jax.random.split(jax.random.key(seed), 8)
    tokens = bell_draw(splits[0], (TOKENS, D), 1.0, 6.0, ((0, 64), (1, 8)))
    out_grad = bell_draw(splits[1], (TOKENS, D), 1.0, 6.0, ((0, 64), (1, 8)))
    gate_up_weight = bell_draw(splits[2], (EXPERTS, D, 2 * FF), D ** -0.5, 0.09375, ((0, 64), (1, 8)))
    down_weight = bell_draw(splits[3], (EXPERTS, FF, D), FF ** -0.5, 0.1875, ((0, 64), (2, 8)))
    routes_keys = jax.random.split(jax.random.fold_in(splits[4], 1), TOKENS // TOK_DEV)
    routes_turns = jax.random.permutation(jax.random.fold_in(splits[4], 3), TOKENS // TOK_DEV)
    routes = jax.vmap(lambda own, number: deal_out(jax.random.fold_in(splits[4], 2), own, number, TOK_DEV, EXPERTS, TOP, CAP, 2))(routes_keys, routes_turns).reshape((TOKENS, TOP))
    route_weight = jnp.clip(jnp.exp(math.log(1.0) - 2.3025851 * jax.random.uniform(splits[5], (TOKENS, TOP), jnp.float32) ** steps_of(splits[5], (TOKENS, TOP), ((0, 64),), -0.2, 0.2)), 0.1, 1.0)
    swapped = draw_swapped(jax.random.fold_in(splits[7], 71), 0)
    return {"tokens": tokens, "out_grad": out_grad, "gate_up_weight": gate_up_weight, "down_weight": down_weight, "routes": routes, "route_weight": route_weight, "swapped": swapped}


def block_sum(left, right, pattern):
    parts = jnp.einsum(pattern, left, right)
    rounded = lax.optimization_barrier(parts.astype(jnp.bfloat16))
    return jnp.sum(rounded.astype(jnp.float32), axis=0)


def reference(tokens, out_grad, gate_up_weight, down_weight, routes, route_weight, swapped):
    total_rows = TOKENS * TOP
    block_rows = TOK_DEV * TOP
    buffer_rows = (TOKENS // TOK_DEV) * CAP
    width_block = D // N_DP
    flat = routes.reshape(-1).astype(jnp.int32)
    column = (jnp.arange(total_rows, dtype=jnp.int32) // block_rows).astype(jnp.int32)
    onehot = (flat[:, None] == jnp.arange(EXPERTS, dtype=jnp.int32)[None, :]).astype(jnp.int32)
    running = jnp.cumsum(onehot.reshape(TOKENS // TOK_DEV, block_rows, EXPERTS), axis=1).reshape(total_rows, EXPERTS)
    slot = jnp.sum(running * onehot, axis=1).astype(jnp.int32) - 1
    spot = flat * buffer_rows + column * CAP + slot
    table = jnp.full((EXPERTS * buffer_rows,), total_rows, jnp.int32)
    table = table.at[spot].set(jnp.arange(total_rows, dtype=jnp.int32)).reshape(EXPERTS, buffer_rows)
    token_pad = jnp.concatenate([tokens, jnp.zeros((1, D), jnp.bfloat16)], axis=0)
    grad_pad = jnp.concatenate([out_grad, jnp.zeros((1, D), jnp.bfloat16)], axis=0)
    weight_pad = jnp.concatenate([route_weight.reshape(-1), jnp.zeros((1,), jnp.float32)], axis=0)

    def per_expert(carry, inputs):
        out_acc, dx_acc = carry
        rows, w_gate_up, w_down = inputs
        token_index = rows // TOP
        weights = weight_pad[rows]
        token_rows = token_pad[token_index]
        row_grad = (weights[:, None] * grad_pad[token_index].astype(jnp.float32)).astype(jnp.bfloat16)
        left = token_rows.astype(jnp.float32).reshape(buffer_rows, N_DP, width_block)
        right = w_gate_up.astype(jnp.float32).reshape(N_DP, width_block, 2 * FF)
        gate_up = block_sum(left, right, "rbk,bkf->brf")
        gate_val = gate_up[:, :FF]
        up_val = gate_up[:, FF:]
        sig = jax.nn.sigmoid(gate_val)
        act = gate_val * sig
        hidden = (act * up_val).astype(jnp.bfloat16)
        row_out = jnp.dot(hidden, w_down, preferred_element_type=jnp.float32).astype(jnp.bfloat16)
        grad_left = row_grad.astype(jnp.float32).reshape(buffer_rows, N_DP, width_block)
        down_right = w_down.astype(jnp.float32).reshape(FF, N_DP, width_block)
        hidden_grad = block_sum(grad_left, down_right, "rbk,fbk->brf")
        gate_grad = hidden_grad * up_val * sig * (1.0 + gate_val * (1.0 - sig))
        up_grad = hidden_grad * act
        gate_up_grad = jnp.concatenate([gate_grad, up_grad], axis=1).astype(jnp.bfloat16)
        row_dx = lax.dot_general(gate_up_grad, w_gate_up, (((1,), (1,)), ((), ())), preferred_element_type=jnp.float32).astype(jnp.bfloat16)
        expert_grad = lax.dot_general(hidden, row_grad, (((0,), (0,)), ((), ())), preferred_element_type=jnp.float32).astype(jnp.bfloat16)
        out_acc = out_acc.at[token_index].add(weights[:, None] * row_out.astype(jnp.float32))
        dx_acc = dx_acc.at[token_index].add(row_dx.astype(jnp.float32))
        return (out_acc, dx_acc), expert_grad

    start = (jnp.zeros((TOKENS + 1, D), jnp.float32), jnp.zeros((TOKENS + 1, D), jnp.float32))
    (out_acc, dx_acc), expert_grad = lax.scan(per_expert, start, (table, gate_up_weight, down_weight))
    layer_out = out_acc[:TOKENS].astype(jnp.bfloat16)
    token_grad = dx_acc[:TOKENS].astype(jnp.bfloat16)
    moved = jnp.any(swapped[:, None] == jnp.arange(PAIRS_ALL, dtype=jnp.int32)[None, :], axis=0)
    device_ids = jnp.arange(EXPERTS, dtype=jnp.int32)
    host = jnp.where(moved[device_ids % PAIRS_ALL], (device_ids + PAIRS_ALL) % EXPERTS, device_ids).astype(jnp.int32)
    down_grad = expert_grad[host]
    return layer_out, token_grad, down_grad
```

```python
import functools

import jax
import jax.numpy as jnp
from jax import lax
from jax.experimental import pallas as pl
from jax.experimental.pallas import tpu as pltpu
from jax.sharding import PartitionSpec as P

MESH = pl.DeviceIdType.MESH
F32 = jnp.float32
BF16 = jnp.bfloat16
SEMS = 80


def dot(a, b, dims):
    return lax.dot_general(a, b, (dims, ((), ())), preferred_element_type=F32)


def kernel(
    experts, cap,
    tok_ref, grad_ref, wg_hbm, wd_hbm, routes_ref, rw_ref, swapped_ref,
    out_ref, dx_ref, dg_hbm,
    wp, wd, st, sg, rt, rg, so, sx, ro, rx, tm, gm, pt,
    pg, xg, sgu, relg, augg, fromg, own,
    ph, xh, sh, relh, augh, fromh,
    hf, gu, eg, er, ed,
    ss, rs, lsem,
):
    dp = lax.axis_index("dp")
    me = lax.axis_index("expert")
    h, c = dp // 2, dp % 2
    tokens, width = tok_ref.shape
    rows = experts * cap
    half = rows // 2
    units = wd.shape[0] // 8
    plus = {"dp": lax.rem(dp + 2, 8)}
    minus = {"dp": lax.rem(dp + 6, 8)}
    other = {"dp": 2 * h + 1 - c}
    top, low = pl.ds(0, half), pl.ds(half, half)

    barrier = pltpu.get_barrier_semaphore()

    def greet(k, carry):
        pl.semaphore_signal(
            barrier, inc=1, device_id={"expert": lax.rem(me + k, experts)}, device_id_type=MESH
        )
        return carry

    for peer in (plus, minus, other):
        pl.semaphore_signal(barrier, inc=1, device_id=peer, device_id_type=MESH)
    lax.fori_loop(1, experts, greet, 0)

    loads = [pltpu.make_async_copy(wd_hbm.at[0], wd, lsem.at[0])]
    for u in range(8):
        for part in range(2):
            loads.append(
                pltpu.make_async_copy(
                    wg_hbm.at[0, :, pl.ds((8 * part + u) * units, units)],
                    wp.at[:, pl.ds((2 * u + part) * units, units)],
                    lsem.at[1 + 2 * u + part],
                )
            )
    for load in loads:
        load.start()

    def remote(src, dst, i, device):
        return pltpu.make_async_remote_copy(
            src_ref=src, dst_ref=dst, send_sem=ss.at[i], recv_sem=rs.at[i],
            device_id=device, device_id_type=MESH,
        )

    def exchange(src, dst, i):
        pltpu.make_async_copy(src.at[me], dst.at[me], rs.at[i]).start()

        def send(k, carry):
            peer = lax.rem(me + k, experts)
            remote(src.at[peer], dst.at[me], i, {"expert": peer}).start()
            return carry

        lax.fori_loop(1, experts, send, 0)

    def arrived(dst, i):
        pltpu.make_async_copy(dst, dst, rs.at[i]).wait()

    def departed(src, i):
        part = src.at[pl.ds(0, experts - 1)]
        remote(part, part, i, {"expert": me}).wait_send()

    lanes = lax.broadcasted_iota(jnp.int32, (tokens, experts), 1)
    named = [jnp.where(routes_ref[:, k : k + 1] == lanes, 1.0, 0.0).astype(BF16) for k in range(2)]
    before = (
        lax.broadcasted_iota(jnp.int32, (tokens, tokens), 1)
        < lax.broadcasted_iota(jnp.int32, (tokens, tokens), 0)
    )
    before = jnp.where(before, 1.0, 0.0).astype(BF16)
    counts = [dot(before, n, ((1,), (0,))) for n in named]
    counts[1] = counts[1] + jnp.sum(named[0].astype(F32), axis=0, keepdims=True)
    places = lax.broadcasted_iota(jnp.int32, (tokens, rows), 1)
    for k in range(2):
        slot = jnp.sum(named[k].astype(F32) * counts[k], axis=1, keepdims=True).astype(jnp.int32)
        spot = routes_ref[:, k : k + 1] * cap + slot
        pt[pl.ds(k * tokens, tokens), :] = jnp.where(spot == places, 1.0, 0.0).astype(BF16)
    both = pt[pl.ds(0, tokens), :] + pt[pl.ds(tokens, tokens), :]
    st[...] = dot(both, tok_ref[...], ((0,), (0,))).reshape(experts, cap, width).astype(BF16)
    pl.semaphore_wait(barrier, experts + 2)
    exchange(st, rt, 0)
    grad = grad_ref[...].astype(F32)
    weighted = jnp.concatenate(
        [(rw_ref[:, k : k + 1] * grad).astype(BF16) for k in range(2)], axis=0
    )
    sg[...] = dot(pt[...], weighted, ((0,), (0,))).reshape(experts, cap, width).astype(BF16)
    exchange(sg, rg, 1)

    def reduce_parts(left, parts, xrecv, sums, rel, frm, base, right, dims, w):
        swaps = {}
        for d in (2, 1, 3, 0):
            j = lax.rem(h + d, 4)
            block = dot(left[...], right(j), dims).astype(BF16)
            parts[d, 0] = block[:, :w]
            parts[d, 1] = block[:, w:]
            swaps[d] = remote(parts.at[d, 1 - c], xrecv.at[d], base + d, other)
            swaps[d].start()
        sent = list(swaps.values())
        for d in (2, 1, 3, 0):
            swaps[d].wait_recv()
            sums[d] = (parts[d, c].astype(F32) + xrecv[d].astype(F32)).astype(BF16)
            if d == 2:
                new = [
                    remote(sums.at[2, top], rel.at[0], base + 4, plus),
                    remote(sums.at[2, low], rel.at[1], base + 5, minus),
                ]
            elif d == 1:
                new = [remote(sums.at[1, low], frm.at[0, low], base + 6, plus)]
            elif d == 3:
                new = [remote(sums.at[3, top], frm.at[1, top], base + 7, minus)]
            else:
                new = []
            for copy in new:
                copy.start()
            sent += new
        return sent

    def reduce_relay(sums, rel, aug, frm, base):
        remote(rel.at[0], rel.at[0], base + 4, plus).wait_recv()
        aug[0] = (sums[1, top].astype(F32) + rel[0].astype(F32)).astype(BF16)
        one = remote(aug.at[0], frm.at[0, top], base + 8, plus)
        one.start()
        remote(rel.at[1], rel.at[1], base + 5, minus).wait_recv()
        aug[1] = (sums[3, low].astype(F32) + rel[1].astype(F32)).astype(BF16)
        two = remote(aug.at[1], frm.at[1, low], base + 9, minus)
        two.start()
        return [one, two]

    def reduce_end(sums, frm, base):
        remote(frm.at[0, low], frm.at[0, low], base + 6, plus).wait_recv()
        remote(frm.at[1, top], frm.at[1, top], base + 7, minus).wait_recv()
        remote(frm.at[0, top], frm.at[0, top], base + 8, plus).wait_recv()
        remote(frm.at[1, low], frm.at[1, low], base + 9, minus).wait_recv()
        return sums[0].astype(F32) + frm[0].astype(F32) + frm[1].astype(F32)

    def block_of(index, w):
        return pl.ds(pl.multiple_of(index * w, w), w)

    u_own = 2 * h + c
    u_plus = 2 * lax.rem(h + 1, 4) + c
    u_minus = 2 * lax.rem(h + 3, 4) + c
    u_far = 2 * lax.rem(h + 2, 4) + c

    def gather_start(buf, w, base):
        mine = block_of(u_own, w)
        new = [
            remote(buf.at[top, mine], buf.at[top, mine], base + 0, plus),
            remote(buf.at[low, mine], buf.at[low, mine], base + 1, minus),
            remote(buf.at[low, mine], buf.at[low, mine], base + 2, plus),
            remote(buf.at[top, mine], buf.at[top, mine], base + 3, minus),
            remote(buf.at[:, mine], buf.at[:, mine], base + 6, other),
        ]
        for copy in new:
            copy.start()
        return new

    def gather_relay(buf, w, base):
        new = []

        def on(rows_of, u, i, device, onward, over):
            ref = buf.at[rows_of, block_of(u, w)]
            remote(ref, ref, base + i, device).wait_recv()
            if onward is not None:
                new.append(remote(ref, ref, base + onward, device))
                new[-1].start()
            new.append(remote(ref, ref, base + over, other))
            new[-1].start()

        on(top, u_minus, 0, plus, 4, 7)
        on(low, u_plus, 1, minus, 5, 8)
        on(low, u_minus, 2, plus, None, 9)
        on(top, u_plus, 3, minus, None, 10)
        return new, on

    def gather_end(buf, w, base, on):
        on(top, u_far, 4, plus, None, 11)
        on(low, u_far, 5, minus, None, 12)
        shift = 1 - 2 * c
        for rows_of, u, i in (
            (slice(None), u_own, 6), (top, u_minus, 7), (low, u_plus, 8), (low, u_minus, 9),
            (top, u_plus, 10), (top, u_far, 11), (low, u_far, 12),
        ):
            ref = buf.at[rows_of, block_of(u + shift, w)]
            remote(ref, ref, base + i, other).wait_recv()

    sent = []
    arrived(rt, 0)
    tm[...] = rt[...].astype(F32).reshape(rows, width).astype(BF16)
    for load in loads:
        load.wait()
    RG, RH, AH, AG = 4, 14, 24, 37
    sent += reduce_parts(
        tm, pg, xg, sgu, relg, fromg, RG,
        lambda j: wp[:, pl.ds(pl.multiple_of(4 * units * j, 4 * units), 4 * units)],
        ((1,), (0,)), 2 * units,
    )
    arrived(rg, 1)
    gm[...] = rg[...].astype(F32).reshape(rows, width).astype(BF16)
    sent += reduce_parts(
        gm, ph, xh, sh, relh, fromh, RH,
        lambda j: wd[pl.ds(pl.multiple_of(2 * units * j, 2 * units), 2 * units), :],
        ((1,), (1,)), units,
    )
    sent += reduce_relay(sgu, relg, augg, fromg, RG)
    sent += reduce_relay(sh, relh, augh, fromh, RH)
    own[...] = reduce_end(sgu, fromg, RG)
    gate, up = own[:, :units], own[:, units:]
    hf[:, block_of(u_own, units)] = (gate * jax.nn.sigmoid(gate) * up).astype(BF16)
    sent += gather_start(hf, units, AH)
    hidden_grad = reduce_end(sh, fromh, RH)
    gate, up = own[:, :units], own[:, units:]
    sig = jax.nn.sigmoid(gate)
    gate_grad = hidden_grad * up * sig * (1.0 + gate * (1.0 - sig))
    up_grad = hidden_grad * (gate * sig)
    gu[:, block_of(u_own, 2 * units)] = jnp.concatenate([gate_grad, up_grad], axis=1).astype(BF16)
    sent += gather_start(gu, 2 * units, AG)
    new, on = gather_relay(hf, units, AH)
    gather_end(hf, units, AH, on)
    sent += new
    so[...] = dot(hf[...], wd[...], ((1,), (0,))).reshape(experts, cap, width).astype(BF16)
    exchange(so, ro, 2)
    eg[...] = dot(hf[...], gm[...], ((0,), (0,))).astype(BF16)
    trade = remote(eg, er, 50, {"expert": lax.rem(me + experts // 2, experts)})
    trade.start()
    new, on = gather_relay(gu, 2 * units, AG)
    gather_end(gu, 2 * units, AG, on)
    sent += new
    sx[...] = dot(gu[...], wp[...], ((1,), (1,))).reshape(experts, cap, width).astype(BF16)
    exchange(sx, rx, 3)
    trade.wait_recv()
    moved = jnp.where(swapped_ref[...] == lax.rem(me, experts // 2), 1.0, 0.0)
    moved = jnp.max(moved, axis=1, keepdims=True)
    ed[...] = jnp.where(moved > 0.5, er[...].astype(F32), eg[...].astype(F32)).astype(BF16)
    store = pltpu.make_async_copy(ed, dg_hbm.at[0], lsem.at[0])
    store.start()
    arrived(ro, 2)
    back = ro[...].astype(F32).reshape(rows, width).astype(BF16)
    total = rw_ref[:, 0:1] * dot(pt[pl.ds(0, tokens), :], back, ((1,), (0,)))
    total = total + rw_ref[:, 1:2] * dot(pt[pl.ds(tokens, tokens), :], back, ((1,), (0,)))
    out_ref[...] = total.astype(BF16)
    arrived(rx, 3)
    both = pt[pl.ds(0, tokens), :] + pt[pl.ds(tokens, tokens), :]
    back = rx[...].astype(F32).reshape(rows, width).astype(BF16)
    dx_ref[...] = dot(both, back, ((1,), (0,))).astype(BF16)
    for copy in sent:
        copy.wait_send()
    trade.wait_send()
    departed(st, 0)
    departed(sg, 1)
    departed(so, 2)
    departed(sx, 3)
    store.wait()


def on_device(tokens, out_grad, gate_up_weight, down_weight, routes, route_weight, swapped):
    experts = lax.axis_size("expert")
    count, width = tokens.shape
    hidden = down_weight.shape[1]
    cap = max(2, 2 * count * routes.shape[1] // experts)
    rows = experts * cap
    units = hidden // 8
    half = rows // 2
    vm = lambda *shape: pltpu.VMEM(shape, BF16)
    scratch = [
        vm(width, 2 * hidden), vm(hidden, width),
        *[vm(experts, cap, width) for _ in range(8)],
        vm(rows, width), vm(rows, width), vm(2 * count, rows),
        vm(4, 2, rows, 2 * units), vm(4, rows, 2 * units), vm(4, rows, 2 * units),
        vm(2, half, 2 * units), vm(2, half, 2 * units), vm(2, rows, 2 * units),
        pltpu.VMEM((rows, 2 * units), F32),
        vm(4, 2, rows, units), vm(4, rows, units), vm(4, rows, units),
        vm(2, half, units), vm(2, half, units), vm(2, rows, units),
        vm(rows, hidden), vm(rows, 2 * hidden),
        vm(hidden, width), vm(hidden, width), vm(hidden, width),
        pltpu.SemaphoreType.DMA((SEMS,)), pltpu.SemaphoreType.DMA((SEMS,)),
        pltpu.SemaphoreType.DMA((17,)),
    ]
    whole = pl.BlockSpec(memory_space=pltpu.VMEM)
    place = pl.BlockSpec(memory_space=pl.ANY)
    return pl.pallas_call(
        functools.partial(kernel, experts, cap),
        out_shape=(
            jax.ShapeDtypeStruct((count, width), BF16),
            jax.ShapeDtypeStruct((count, width), BF16),
            jax.ShapeDtypeStruct(down_weight.shape, BF16),
        ),
        in_specs=[whole, whole, place, place, whole, whole, whole],
        out_specs=(whole, whole, place),
        scratch_shapes=scratch,
        compiler_params=pltpu.CompilerParams(collective_id=0, has_side_effects=True),
        name="layer",
    )(tokens, out_grad, gate_up_weight, down_weight, routes, route_weight, swapped.reshape(1, -1))


def solution(mesh):
    return jax.shard_map(
        on_device,
        mesh=mesh,
        in_specs=(
            P("expert", "dp"),
            P("expert", "dp"),
            P("expert", "dp", None),
            P("expert", None, "dp"),
            P("expert", None),
            P("expert", None),
            P(),
        ),
        out_specs=(P("expert", "dp"), P("expert", "dp"), P("expert", None, "dp")),
        check_vma=False,
    )
```

```python
import functools

import jax
import jax.numpy as jnp
from jax import lax
from jax.experimental import pallas as pl
from jax.experimental.pallas import tpu as pltpu
from jax.sharding import PartitionSpec as P

MESH = pl.DeviceIdType.MESH
F32 = jnp.float32
BF16 = jnp.bfloat16
SEMS = 80


def dot(a, b, dims):
    return lax.dot_general(a, b, (dims, ((), ())), preferred_element_type=F32)


def kernel(
    experts, cap,
    tok_hbm, grad_hbm, wg_hbm, wd_hbm, routes_hbm, rw_hbm, swapped_hbm,
    out_ref, dx_ref, dg_hbm,
    tok_ref, grad_ref, routes_ref, rw_ref, swapped_ref,
    wp, wd, xt, st, sg, rt, rg, so, sx, ro, rx, tm, gm, sel,
    pg, xg, sgu, relg, augg, fromg, own,
    ph, xh, sh, relh, augh, fromh,
    hf, gu, eg, er, ed,
    ss, rs, lsem,
):
    dp = lax.axis_index("dp")
    me = lax.axis_index("expert")
    h, c = dp // 2, dp % 2
    width, tokens = tok_ref.shape
    body = width // 128 * 128
    rest = width - body
    rows = experts * cap
    half = rows // 2
    units = wd.shape[1] // 8
    plus = {"dp": lax.rem(dp + 2, 8)}
    minus = {"dp": lax.rem(dp + 6, 8)}
    other = {"dp": 2 * h + 1 - c}
    top, low = pl.ds(0, half), pl.ds(half, half)

    barrier = pltpu.get_barrier_semaphore()

    def greet(k, carry):
        pl.semaphore_signal(
            barrier, inc=1, device_id={"expert": lax.rem(me + k, experts)}, device_id_type=MESH
        )
        return carry

    for peer in (plus, minus, other):
        pl.semaphore_signal(barrier, inc=1, device_id=peer, device_id_type=MESH)
    lax.fori_loop(1, experts, greet, 0)

    small = [
        pltpu.make_async_copy(src, dst, lsem.at[17 + i])
        for i, (src, dst) in enumerate((
            (routes_hbm, routes_ref), (tok_hbm, tok_ref), (grad_hbm, grad_ref), (rw_hbm, rw_ref),
            (swapped_hbm, swapped_ref),
        ))
    ]
    for load in small:
        load.start()
    loads = [pltpu.make_async_copy(wd_hbm.at[0], wd, lsem.at[0])]
    for u in range(8):
        for part in range(2):
            loads.append(
                pltpu.make_async_copy(
                    wg_hbm.at[0, :, pl.ds((8 * part + u) * units, units)],
                    wp.at[:, pl.ds((2 * u + part) * units, units)],
                    lsem.at[1 + 2 * u + part],
                )
            )
    for load in loads:
        load.start()

    def remote(src, dst, i, device):
        return pltpu.make_async_remote_copy(
            src_ref=src, dst_ref=dst, send_sem=ss.at[i], recv_sem=rs.at[i],
            device_id=device, device_id_type=MESH,
        )

    def exchange(src, dst, i):
        pltpu.make_async_copy(src.at[me], dst.at[me], rs.at[i]).start()

        def send(k, carry):
            peer = lax.rem(me + k, experts)
            remote(src.at[peer], dst.at[me], i, {"expert": peer}).start()
            return carry

        lax.fori_loop(1, experts, send, 0)

    def arrived(dst, i):
        pltpu.make_async_copy(dst, dst, rs.at[i]).wait()

    def departed(src, i):
        part = src.at[pl.ds(0, experts - 1)]
        remote(part, part, i, {"expert": me}).wait_send()

    for load in small:
        load.wait()
    ids = lax.broadcasted_iota(jnp.int32, (experts, tokens), 0)
    named = [jnp.where(routes_ref[k : k + 1, :] == ids, 1.0, 0.0) for k in range(2)]
    before = (
        lax.broadcasted_iota(jnp.int32, (tokens, tokens), 0)
        < lax.broadcasted_iota(jnp.int32, (tokens, tokens), 1)
    )
    before = jnp.where(before, 1.0, 0.0).astype(BF16)
    counts = [dot(n.astype(BF16), before, ((1,), (0,))) for n in named]
    counts[1] = counts[1] + jnp.sum(named[0], axis=1, keepdims=True)
    places = lax.broadcasted_iota(jnp.int32, (rows, tokens), 0)
    grad = grad_ref[...].astype(F32)
    for k in range(2):
        of = pl.ds(k * tokens, tokens)
        slot = jnp.sum(named[k] * counts[k], axis=0, keepdims=True).astype(jnp.int32)
        spot = routes_ref[k : k + 1, :] * cap + slot
        sel[:, of] = jnp.where(spot == places, 1.0, 0.0).astype(BF16)
        xt[pl.ds(0, width), of] = tok_ref[...]
        weighted = (rw_ref[k : k + 1, :] * grad).astype(BF16)
        xt[pl.ds(width, rest), of] = weighted[body:]
        xt[pl.ds(width + rest, body), of] = weighted[:body]
    full = width + rest
    st[...] = dot(sel[...], xt[pl.ds(0, full), :], ((1,), (1,))).reshape(experts, cap, full).astype(BF16)
    pl.semaphore_wait(barrier, experts + 2)
    exchange(st, rt, 0)
    sg[...] = dot(sel[...], xt[pl.ds(full, body), :], ((1,), (1,))).reshape(experts, cap, body).astype(BF16)
    exchange(sg, rg, 1)

    def reduce_parts(left, parts, xrecv, sums, rel, frm, base, right, dims, w):
        swaps = {}
        for d in (2, 1, 3, 0):
            j = lax.rem(h + d, 4)
            block = dot(left[...], right(j), dims).astype(BF16)
            parts[d, 0] = block[:, :w]
            parts[d, 1] = block[:, w:]
            swaps[d] = remote(parts.at[d, 1 - c], xrecv.at[d], base + d, other)
            swaps[d].start()
        sent = list(swaps.values())
        for d in (2, 1, 3, 0):
            swaps[d].wait_recv()
            sums[d] = (parts[d, c].astype(F32) + xrecv[d].astype(F32)).astype(BF16)
            if d == 2:
                new = [
                    remote(sums.at[2, top], rel.at[0], base + 4, plus),
                    remote(sums.at[2, low], rel.at[1], base + 5, minus),
                ]
            elif d == 1:
                new = [remote(sums.at[1, low], frm.at[0, low], base + 6, plus)]
            elif d == 3:
                new = [remote(sums.at[3, top], frm.at[1, top], base + 7, minus)]
            else:
                new = []
            for copy in new:
                copy.start()
            sent += new
        return sent

    def reduce_relay(sums, rel, aug, frm, base):
        remote(rel.at[0], rel.at[0], base + 4, plus).wait_recv()
        aug[0] = (sums[1, top].astype(F32) + rel[0].astype(F32)).astype(BF16)
        one = remote(aug.at[0], frm.at[0, top], base + 8, plus)
        one.start()
        remote(rel.at[1], rel.at[1], base + 5, minus).wait_recv()
        aug[1] = (sums[3, low].astype(F32) + rel[1].astype(F32)).astype(BF16)
        two = remote(aug.at[1], frm.at[1, low], base + 9, minus)
        two.start()
        return [one, two]

    def reduce_end(sums, frm, base):
        remote(frm.at[0, low], frm.at[0, low], base + 6, plus).wait_recv()
        remote(frm.at[1, top], frm.at[1, top], base + 7, minus).wait_recv()
        remote(frm.at[0, top], frm.at[0, top], base + 8, plus).wait_recv()
        remote(frm.at[1, low], frm.at[1, low], base + 9, minus).wait_recv()
        return sums[0].astype(F32) + frm[0].astype(F32) + frm[1].astype(F32)

    def block_of(index, w):
        return pl.ds(pl.multiple_of(index * w, w), w)

    u_own = 2 * h + c
    u_plus = 2 * lax.rem(h + 1, 4) + c
    u_minus = 2 * lax.rem(h + 3, 4) + c
    u_far = 2 * lax.rem(h + 2, 4) + c

    def put(sent, src, dst, i, device):
        copy = remote(src, dst, i, device)
        copy.start()
        sent.append(copy)

    def gather_first(sent, buf, w, base):
        mine = block_of(u_own, w)
        put(sent, buf.at[top, mine], buf.at[top, mine], base + 0, plus)
        put(sent, buf.at[low, mine], buf.at[low, mine], base + 1, minus)

    def gather_second(sent, buf, w, base):
        mine = block_of(u_own, w)
        put(sent, buf.at[low, mine], buf.at[low, mine], base + 2, plus)
        put(sent, buf.at[top, mine], buf.at[top, mine], base + 3, minus)
        put(sent, buf.at[:, mine], buf.at[:, mine], base + 6, other)

    def gather_on(sent, buf, w, base, steps):
        for rows_of, u, i, device, onward, over in steps:
            ref = buf.at[rows_of, block_of(u, w)]
            remote(ref, ref, base + i, device).wait_recv()
            if onward is not None:
                put(sent, ref, ref, base + onward, device)
            put(sent, ref, ref, base + over, other)

    on_first = ((top, u_minus, 0, plus, 4, 7), (low, u_plus, 1, minus, 5, 8))
    on_second = ((low, u_minus, 2, plus, None, 9), (top, u_plus, 3, minus, None, 10))
    on_last = ((top, u_far, 4, plus, None, 11), (low, u_far, 5, minus, None, 12))

    def gather_end(buf, w, base):
        shift = 1 - 2 * c
        for rows_of, u, i in (
            (slice(None), u_own, 6), (top, u_minus, 7), (low, u_plus, 8), (low, u_minus, 9),
            (top, u_plus, 10), (top, u_far, 11), (low, u_far, 12),
        ):
            ref = buf.at[rows_of, block_of(u + shift, w)]
            remote(ref, ref, base + i, other).wait_recv()

    sent = []
    arrived(rt, 0)
    came = rt[...].astype(F32).reshape(rows, full)
    tm[...] = came[:, :width].astype(BF16)
    gm[:, body:] = came[:, width:].astype(BF16)
    for load in loads:
        load.wait()
    RG, RH, AH, AG = 4, 14, 24, 37
    sent += reduce_parts(
        tm, pg, xg, sgu, relg, fromg, RG,
        lambda j: wp[:, pl.ds(pl.multiple_of(4 * units * j, 4 * units), 4 * units)],
        ((1,), (0,)), 2 * units,
    )
    arrived(rg, 1)
    gm[:, :body] = rg[...].astype(F32).reshape(rows, body).astype(BF16)
    sent += reduce_parts(
        gm, ph, xh, sh, relh, fromh, RH,
        lambda j: wd[:, pl.ds(pl.multiple_of(2 * units * j, 2 * units), 2 * units)],
        ((1,), (0,)), units,
    )
    sent += reduce_relay(sgu, relg, augg, fromg, RG)
    sent += reduce_relay(sh, relh, augh, fromh, RH)
    own[...] = reduce_end(sgu, fromg, RG)
    gate, up = own[:, :units], own[:, units:]
    hf[:, block_of(u_own, units)] = (gate * jax.nn.sigmoid(gate) * up).astype(BF16)
    gather_first(sent, hf, units, AH)
    gather_second(sent, hf, units, AH)
    hidden_grad = reduce_end(sh, fromh, RH)
    gate, up = own[:, :units], own[:, units:]
    sig = jax.nn.sigmoid(gate)
    gate_grad = hidden_grad * up * sig * (1.0 + gate * (1.0 - sig))
    up_grad = hidden_grad * (gate * sig)
    gu[:, block_of(u_own, 2 * units)] = jnp.concatenate([gate_grad, up_grad], axis=1).astype(BF16)
    gather_first(sent, gu, 2 * units, AG)
    gather_on(sent, hf, units, AH, on_first)
    gather_second(sent, gu, 2 * units, AG)
    gather_on(sent, hf, units, AH, on_second)
    gather_on(sent, gu, 2 * units, AG, on_first)
    gather_on(sent, hf, units, AH, on_last)
    gather_end(hf, units, AH)
    row_out = dot(hf[...], wd[...], ((1,), (1,)))
    so[...] = row_out[:, :body].reshape(experts, cap, body).astype(BF16)
    sx[:, :, width:] = row_out[:, body:].reshape(experts, cap, rest).astype(BF16)
    eg[...] = dot(gm[...], hf[...], ((0,), (0,))).astype(BF16)
    trade = remote(eg, er, 50, {"expert": lax.rem(me + experts // 2, experts)})
    trade.start()
    gather_on(sent, gu, 2 * units, AG, on_second)
    exchange(so, ro, 2)
    gather_on(sent, gu, 2 * units, AG, on_last)
    gather_end(gu, 2 * units, AG)
    sx[:, :, :width] = dot(gu[...], wp[...], ((1,), (1,))).reshape(experts, cap, width).astype(BF16)
    exchange(sx, rx, 3)
    trade.wait_recv()
    moved = jnp.where(swapped_ref[...] == lax.rem(me, experts // 2), 1.0, 0.0)
    moved = jnp.max(moved, axis=1, keepdims=True)
    ed[...] = jnp.where(moved > 0.5, er[...].astype(F32), eg[...].astype(F32)).astype(BF16)
    store = pltpu.make_async_copy(ed, dg_hbm.at[0], lsem.at[0])
    store.start()

    def combined(both):
        first, second = both[:, :tokens], both[:, tokens:]
        return rw_ref[0:1, :] * first + rw_ref[1:2, :] * second

    arrived(ro, 2)
    back = ro[...].astype(F32).reshape(rows, body).astype(BF16)
    out_ref[pl.ds(0, body), :] = combined(dot(back, sel[...], ((0,), (0,)))).astype(BF16)
    arrived(rx, 3)
    back = rx[...].astype(F32).reshape(rows, full).astype(BF16)
    both = dot(back, sel[...], ((0,), (0,)))
    out_ref[pl.ds(body, rest), :] = combined(both[width:]).astype(BF16)
    dx_ref[...] = (both[:width, :tokens] + both[:width, tokens:]).astype(BF16)
    for copy in sent:
        copy.wait_send()
    trade.wait_send()
    departed(st, 0)
    departed(sg, 1)
    departed(so, 2)
    departed(sx, 3)
    store.wait()


def on_device(tokens, out_grad, gate_up_weight, down_weight, routes, route_weight, swapped):
    experts = lax.axis_size("expert")
    count, width = tokens.shape
    hidden = down_weight.shape[1]
    cap = max(2, 2 * count * routes.shape[1] // experts)
    rows = experts * cap
    units = hidden // 8
    half = rows // 2
    body = width // 128 * 128
    full = 2 * width - body
    vm = lambda *shape: pltpu.VMEM(shape, BF16)
    scratch = [
        vm(width, count), vm(width, count), pltpu.VMEM((routes.shape[1], count), jnp.int32),
        pltpu.VMEM((routes.shape[1], count), F32), pltpu.VMEM((1, swapped.shape[0]), jnp.int32),
        vm(width, 2 * hidden), vm(width, hidden), vm(2 * width, 2 * count),
        *[vm(experts, cap, w) for w in (full, body, full, body, body, full, body, full)],
        vm(rows, width), vm(rows, width), vm(rows, 2 * count),
        vm(4, 2, rows, 2 * units), vm(4, rows, 2 * units), vm(4, rows, 2 * units),
        vm(2, half, 2 * units), vm(2, half, 2 * units), vm(2, rows, 2 * units),
        pltpu.VMEM((rows, 2 * units), F32),
        vm(4, 2, rows, units), vm(4, rows, units), vm(4, rows, units),
        vm(2, half, units), vm(2, half, units), vm(2, rows, units),
        vm(rows, hidden), vm(rows, 2 * hidden),
        vm(width, hidden), vm(width, hidden), vm(width, hidden),
        pltpu.SemaphoreType.DMA((SEMS,)), pltpu.SemaphoreType.DMA((SEMS,)),
        pltpu.SemaphoreType.DMA((22,)),
    ]
    whole = pl.BlockSpec(memory_space=pltpu.VMEM)
    place = pl.BlockSpec(memory_space=pl.ANY)
    layer_out, token_grad, down_grad = pl.pallas_call(
        functools.partial(kernel, experts, cap),
        out_shape=(
            pltpu.VMEM((width, count), BF16),
            pltpu.VMEM((width, count), BF16),
            pltpu.VMEM((1, width, hidden), BF16),
        ),
        in_specs=[place] * 7,
        out_specs=(whole, whole, place),
        scratch_shapes=scratch,
        compiler_params=pltpu.CompilerParams(collective_id=0, has_side_effects=True, vmem_limit_bytes=58 * 1024 * 1024),
        name="layer",
    )(
        tokens.T, out_grad.T, gate_up_weight, down_weight.transpose(0, 2, 1), routes.T,
        route_weight.T, swapped.reshape(1, -1),
    )
    return layer_out.T, token_grad.T, down_grad.transpose(0, 2, 1)


def solution(mesh):
    return jax.shard_map(
        on_device,
        mesh=mesh,
        in_specs=(
            P("expert", "dp"),
            P("expert", "dp"),
            P("expert", "dp", None),
            P("expert", None, "dp"),
            P("expert", None),
            P("expert", None),
            P(),
        ),
        out_specs=(P("expert", "dp"), P("expert", "dp"), P("expert", None, "dp")),
        check_vma=False,
    )
```

```python
import functools

import jax
import jax.numpy as jnp
from jax import lax
from jax.experimental import pallas as pl
from jax.experimental.pallas import tpu as pltpu
from jax.sharding import PartitionSpec as P

MESH = pl.DeviceIdType.MESH
F32 = jnp.float32
BF16 = jnp.bfloat16
SEMS = 80


def dot(a, b, dims):
    return lax.dot_general(a, b, (dims, ((), ())), preferred_element_type=F32)


def kernel(
    experts, cap,
    tok_hbm, grad_hbm, wg_hbm, wd_hbm, routes_hbm, rw_hbm, swapped_hbm,
    out_ref, dx_ref, dg_hbm,
    tok_ref, grad_ref, routes_ref, rw_ref, swapped_ref,
    wp, wd, xt, st, sg, rt, rg, so, sx, ro, rx, tm, gm, sel,
    pg, xg, sgu, relg, augg, fromg, own,
    ph, xh, sh, relh, augh, fromh,
    hf, gu, eg, er, ed, acc,
    ss, rs, lsem,
):
    dp = lax.axis_index("dp")
    me = lax.axis_index("expert")
    h, c = dp // 2, dp % 2
    width, tokens = tok_ref.shape
    body = width // 128 * 128
    rest = width - body
    rows = experts * cap
    half = rows // 2
    units = wd.shape[1] // 8
    plus = {"dp": lax.rem(dp + 2, 8)}
    minus = {"dp": lax.rem(dp + 6, 8)}
    other = {"dp": 2 * h + 1 - c}
    top, low = pl.ds(0, half), pl.ds(half, half)

    barrier = pltpu.get_barrier_semaphore()

    def greet(k, carry):
        pl.semaphore_signal(
            barrier, inc=1, device_id={"expert": lax.rem(me + k, experts)}, device_id_type=MESH
        )
        return carry

    for peer in (plus, minus, other):
        pl.semaphore_signal(barrier, inc=1, device_id=peer, device_id_type=MESH)
    lax.fori_loop(1, experts, greet, 0)

    small = [
        pltpu.make_async_copy(src, dst, lsem.at[17 + i])
        for i, (src, dst) in enumerate((
            (routes_hbm, routes_ref), (tok_hbm, tok_ref), (grad_hbm, grad_ref), (rw_hbm, rw_ref),
            (swapped_hbm, swapped_ref),
        ))
    ]
    for load in small:
        load.start()
    loads = [pltpu.make_async_copy(wd_hbm.at[0], wd, lsem.at[0])]
    for u in range(8):
        for part in range(2):
            loads.append(
                pltpu.make_async_copy(
                    wg_hbm.at[0, :, pl.ds((8 * part + u) * units, units)],
                    wp.at[:, pl.ds((2 * u + part) * units, units)],
                    lsem.at[1 + 2 * u + part],
                )
            )
    for load in loads:
        load.start()

    def remote(src, dst, i, device):
        return pltpu.make_async_remote_copy(
            src_ref=src, dst_ref=dst, send_sem=ss.at[i], recv_sem=rs.at[i],
            device_id=device, device_id_type=MESH,
        )

    def exchange(src, dst, i):
        pltpu.make_async_copy(src.at[me], dst.at[me], rs.at[i]).start()

        def send(k, carry):
            peer = lax.rem(me + k, experts)
            remote(src.at[peer], dst.at[me], i, {"expert": peer}).start()
            return carry

        lax.fori_loop(1, experts, send, 0)

    def arrived(dst, i):
        pltpu.make_async_copy(dst, dst, rs.at[i]).wait()

    def departed(src, i):
        part = src.at[pl.ds(0, experts - 1)]
        remote(part, part, i, {"expert": me}).wait_send()

    for load in small:
        load.wait()
    ids = lax.broadcasted_iota(jnp.int32, (experts, tokens), 0)
    named = [jnp.where(routes_ref[k : k + 1, :] == ids, 1.0, 0.0) for k in range(2)]
    before = (
        lax.broadcasted_iota(jnp.int32, (tokens, tokens), 0)
        < lax.broadcasted_iota(jnp.int32, (tokens, tokens), 1)
    )
    before = jnp.where(before, 1.0, 0.0).astype(BF16)
    counts = [dot(n.astype(BF16), before, ((1,), (0,))) for n in named]
    counts[1] = counts[1] + jnp.sum(named[0], axis=1, keepdims=True)
    places = lax.broadcasted_iota(jnp.int32, (rows, tokens), 0)
    grad = grad_ref[...].astype(F32)
    for k in range(2):
        of = pl.ds(k * tokens, tokens)
        slot = jnp.sum(named[k] * counts[k], axis=0, keepdims=True).astype(jnp.int32)
        spot = routes_ref[k : k + 1, :] * cap + slot
        sel[:, of] = jnp.where(spot == places, 1.0, 0.0).astype(BF16)
        xt[pl.ds(0, width), of] = tok_ref[...]
        weighted = (rw_ref[k : k + 1, :] * grad).astype(BF16)
        xt[pl.ds(width, rest), of] = weighted[body:]
        xt[pl.ds(width + rest, body), of] = weighted[:body]
    full = width + rest
    st[...] = dot(sel[...], xt[pl.ds(0, full), :], ((1,), (1,))).reshape(experts, cap, full).astype(BF16)
    pl.semaphore_wait(barrier, experts + 2)
    exchange(st, rt, 0)
    sg[...] = dot(sel[...], xt[pl.ds(full, body), :], ((1,), (1,))).reshape(experts, cap, body).astype(BF16)
    exchange(sg, rg, 1)

    def reduce_parts(left, parts, xrecv, sums, rel, frm, base, right, dims, w):
        swaps = {}
        for d in (2, 1, 3, 0):
            j = lax.rem(h + d, 4)
            block = dot(left[...], right(j), dims).astype(BF16)
            parts[d, 0] = block[:, :w]
            parts[d, 1] = block[:, w:]
            swaps[d] = remote(parts.at[d, 1 - c], xrecv.at[d], base + d, other)
            swaps[d].start()
        sent = list(swaps.values())
        for d in (2, 1, 3, 0):
            swaps[d].wait_recv()
            sums[d] = (parts[d, c].astype(F32) + xrecv[d].astype(F32)).astype(BF16)
            if d == 2:
                new = [
                    remote(sums.at[2, top], rel.at[0], base + 4, plus),
                    remote(sums.at[2, low], rel.at[1], base + 5, minus),
                ]
            elif d == 1:
                new = [remote(sums.at[1, low], frm.at[0, low], base + 6, plus)]
            elif d == 3:
                new = [remote(sums.at[3, top], frm.at[1, top], base + 7, minus)]
            else:
                new = []
            for copy in new:
                copy.start()
            sent += new
        return sent

    def reduce_relay(sums, rel, aug, frm, base):
        remote(rel.at[0], rel.at[0], base + 4, plus).wait_recv()
        aug[0] = (sums[1, top].astype(F32) + rel[0].astype(F32)).astype(BF16)
        one = remote(aug.at[0], frm.at[0, top], base + 8, plus)
        one.start()
        remote(rel.at[1], rel.at[1], base + 5, minus).wait_recv()
        aug[1] = (sums[3, low].astype(F32) + rel[1].astype(F32)).astype(BF16)
        two = remote(aug.at[1], frm.at[1, low], base + 9, minus)
        two.start()
        return [one, two]

    def reduce_end(sums, frm, base):
        remote(frm.at[0, low], frm.at[0, low], base + 6, plus).wait_recv()
        remote(frm.at[1, top], frm.at[1, top], base + 7, minus).wait_recv()
        remote(frm.at[0, top], frm.at[0, top], base + 8, plus).wait_recv()
        remote(frm.at[1, low], frm.at[1, low], base + 9, minus).wait_recv()
        return sums[0].astype(F32) + frm[0].astype(F32) + frm[1].astype(F32)

    def block_of(index, w):
        return pl.ds(pl.multiple_of(index * w, w), w)

    u_own = 2 * h + c
    u_plus = 2 * lax.rem(h + 1, 4) + c
    u_minus = 2 * lax.rem(h + 3, 4) + c
    u_far = 2 * lax.rem(h + 2, 4) + c

    def put(sent, src, dst, i, device):
        copy = remote(src, dst, i, device)
        copy.start()
        sent.append(copy)

    def gather_first(sent, buf, w, base):
        mine = block_of(u_own, w)
        put(sent, buf.at[top, mine], buf.at[top, mine], base + 0, plus)
        put(sent, buf.at[low, mine], buf.at[low, mine], base + 1, minus)

    def gather_second(sent, buf, w, base):
        mine = block_of(u_own, w)
        put(sent, buf.at[low, mine], buf.at[low, mine], base + 2, plus)
        put(sent, buf.at[top, mine], buf.at[top, mine], base + 3, minus)
        put(sent, buf.at[:, mine], buf.at[:, mine], base + 6, other)

    def gather_on(sent, buf, w, base, steps):
        for rows_of, u, i, device, onward, over in steps:
            ref = buf.at[rows_of, block_of(u, w)]
            remote(ref, ref, base + i, device).wait_recv()
            if onward is not None:
                put(sent, ref, ref, base + onward, device)
            put(sent, ref, ref, base + over, other)

    on_first = ((top, u_minus, 0, plus, 4, 7), (low, u_plus, 1, minus, 5, 8))
    on_second = ((low, u_minus, 2, plus, None, 9), (top, u_plus, 3, minus, None, 10))
    on_last = ((top, u_far, 4, plus, None, 11), (low, u_far, 5, minus, None, 12))

    over_own = ((slice(None), u_own, 6),)
    over_near = ((top, u_minus, 7), (low, u_minus, 9), (low, u_plus, 8), (top, u_plus, 10))
    over_far = ((top, u_far, 11), (low, u_far, 12))

    def gather_over(buf, w, base, steps):
        for rows_of, u, i in steps:
            ref = buf.at[rows_of, block_of(u + 1 - 2 * c, w)]
            remote(ref, ref, base + i, other).wait_recv()

    def chip(d, w):
        return block_of(lax.rem(h + d, 4), w)

    trades = []

    def trade(d):
        cols = chip(d, 2 * units)
        eg[:, cols] = dot(gm[...], hf[:, cols], ((0,), (0,))).astype(BF16)
        copy = remote(
            eg.at[:, cols], er.at[:, cols], 50 + d,
            {"expert": lax.rem(me + experts // 2, experts)},
        )
        copy.start()
        trades.append(copy)

    def dx_part(d):
        cols = chip(d, 4 * units)
        return dot(gu[:, cols], wp[:, cols], ((1,), (1,)))

    sent = []
    arrived(rt, 0)
    came = rt[...].astype(F32).reshape(rows, full)
    tm[...] = came[:, :width].astype(BF16)
    gm[:, body:] = came[:, width:].astype(BF16)
    for load in loads:
        load.wait()
    RG, RH, AH, AG = 4, 14, 24, 37
    sent += reduce_parts(
        tm, pg, xg, sgu, relg, fromg, RG,
        lambda j: wp[:, pl.ds(pl.multiple_of(4 * units * j, 4 * units), 4 * units)],
        ((1,), (0,)), 2 * units,
    )
    arrived(rg, 1)
    gm[:, :body] = rg[...].astype(F32).reshape(rows, body).astype(BF16)
    sent += reduce_parts(
        gm, ph, xh, sh, relh, fromh, RH,
        lambda j: wd[:, pl.ds(pl.multiple_of(2 * units * j, 2 * units), 2 * units)],
        ((1,), (0,)), units,
    )
    sent += reduce_relay(sgu, relg, augg, fromg, RG)
    sent += reduce_relay(sh, relh, augh, fromh, RH)
    own[...] = reduce_end(sgu, fromg, RG)
    gate, up = own[:, :units], own[:, units:]
    hf[:, block_of(u_own, units)] = (gate * jax.nn.sigmoid(gate) * up).astype(BF16)
    gather_first(sent, hf, units, AH)
    gather_second(sent, hf, units, AH)
    gather_over(hf, units, AH, over_own)
    trade(0)
    hidden_grad = reduce_end(sh, fromh, RH)
    gate, up = own[:, :units], own[:, units:]
    sig = jax.nn.sigmoid(gate)
    gate_grad = hidden_grad * up * sig * (1.0 + gate * (1.0 - sig))
    up_grad = hidden_grad * (gate * sig)
    gu[:, block_of(u_own, 2 * units)] = jnp.concatenate([gate_grad, up_grad], axis=1).astype(BF16)
    gather_first(sent, gu, 2 * units, AG)
    gather_on(sent, hf, units, AH, on_first)
    gather_second(sent, gu, 2 * units, AG)
    gather_on(sent, hf, units, AH, on_second)
    gather_over(hf, units, AH, over_near)
    trade(1)
    trade(3)
    gather_over(gu, 2 * units, AG, over_own)
    acc[...] = dx_part(0)
    gather_on(sent, gu, 2 * units, AG, on_first)
    gather_on(sent, hf, units, AH, on_last)
    gather_over(hf, units, AH, over_far)
    trade(2)
    row_out = dot(hf[...], wd[...], ((1,), (1,)))
    so[...] = row_out[:, :body].reshape(experts, cap, body).astype(BF16)
    sx[:, :, width:] = row_out[:, body:].reshape(experts, cap, rest).astype(BF16)
    gather_on(sent, gu, 2 * units, AG, on_second)
    exchange(so, ro, 2)
    gather_over(gu, 2 * units, AG, over_near)
    acc[...] = acc[...] + dx_part(1) + dx_part(3)
    gather_on(sent, gu, 2 * units, AG, on_last)
    gather_over(gu, 2 * units, AG, over_far)
    sx[:, :, :width] = (acc[...] + dx_part(2)).reshape(experts, cap, width).astype(BF16)
    exchange(sx, rx, 3)
    for copy in trades:
        copy.wait_recv()
    moved = jnp.where(swapped_ref[...] == lax.rem(me, experts // 2), 1.0, 0.0)
    moved = jnp.max(moved, axis=1, keepdims=True)
    ed[...] = jnp.where(moved > 0.5, er[...].astype(F32), eg[...].astype(F32)).astype(BF16)
    store = pltpu.make_async_copy(ed, dg_hbm.at[0], lsem.at[0])
    store.start()

    def combined(both):
        first, second = both[:, :tokens], both[:, tokens:]
        return rw_ref[0:1, :] * first + rw_ref[1:2, :] * second

    arrived(ro, 2)
    back = ro[...].astype(F32).reshape(rows, body).astype(BF16)
    out_ref[pl.ds(0, body), :] = combined(dot(back, sel[...], ((0,), (0,)))).astype(BF16)
    arrived(rx, 3)
    back = rx[...].astype(F32).reshape(rows, full).astype(BF16)
    both = dot(back, sel[...], ((0,), (0,)))
    out_ref[pl.ds(body, rest), :] = combined(both[width:]).astype(BF16)
    dx_ref[...] = (both[:width, :tokens] + both[:width, tokens:]).astype(BF16)
    for copy in sent:
        copy.wait_send()
    for copy in trades:
        copy.wait_send()
    departed(st, 0)
    departed(sg, 1)
    departed(so, 2)
    departed(sx, 3)
    store.wait()


def on_device(tokens, out_grad, gate_up_weight, down_weight, routes, route_weight, swapped):
    experts = lax.axis_size("expert")
    count, width = tokens.shape
    hidden = down_weight.shape[1]
    cap = max(2, 2 * count * routes.shape[1] // experts)
    rows = experts * cap
    units = hidden // 8
    half = rows // 2
    body = width // 128 * 128
    full = 2 * width - body
    vm = lambda *shape: pltpu.VMEM(shape, BF16)
    scratch = [
        vm(width, count), vm(width, count), pltpu.VMEM((routes.shape[1], count), jnp.int32),
        pltpu.VMEM((routes.shape[1], count), F32), pltpu.VMEM((1, swapped.shape[0]), jnp.int32),
        vm(width, 2 * hidden), vm(width, hidden), vm(2 * width, 2 * count),
        *[vm(experts, cap, w) for w in (full, body, full, body, body, full, body, full)],
        vm(rows, width), vm(rows, width), vm(rows, 2 * count),
        vm(4, 2, rows, 2 * units), vm(4, rows, 2 * units), vm(4, rows, 2 * units),
        vm(2, half, 2 * units), vm(2, half, 2 * units), vm(2, rows, 2 * units),
        pltpu.VMEM((rows, 2 * units), F32),
        vm(4, 2, rows, units), vm(4, rows, units), vm(4, rows, units),
        vm(2, half, units), vm(2, half, units), vm(2, rows, units),
        vm(rows, hidden), vm(rows, 2 * hidden),
        vm(width, hidden), vm(width, hidden), vm(width, hidden),
        pltpu.VMEM((rows, width), F32),
        pltpu.SemaphoreType.DMA((SEMS,)), pltpu.SemaphoreType.DMA((SEMS,)),
        pltpu.SemaphoreType.DMA((22,)),
    ]
    whole = pl.BlockSpec(memory_space=pltpu.VMEM)
    place = pl.BlockSpec(memory_space=pl.ANY)
    layer_out, token_grad, down_grad = pl.pallas_call(
        functools.partial(kernel, experts, cap),
        out_shape=(
            pltpu.VMEM((width, count), BF16),
            pltpu.VMEM((width, count), BF16),
            pltpu.VMEM((1, width, hidden), BF16),
        ),
        in_specs=[place] * 7,
        out_specs=(whole, whole, place),
        scratch_shapes=scratch,
        compiler_params=pltpu.CompilerParams(collective_id=0, has_side_effects=True, vmem_limit_bytes=58 * 1024 * 1024),
        name="layer",
    )(
        tokens.T, out_grad.T, gate_up_weight, down_weight.transpose(0, 2, 1), routes.T,
        route_weight.T, swapped.reshape(1, -1),
    )
    return layer_out.T, token_grad.T, down_grad.transpose(0, 2, 1)


def solution(mesh):
    return jax.shard_map(
        on_device,
        mesh=mesh,
        in_specs=(
            P("expert", "dp"),
            P("expert", "dp"),
            P("expert", "dp", None),
            P("expert", None, "dp"),
            P("expert", None),
            P("expert", None),
            P(),
        ),
        out_specs=(P("expert", "dp"), P("expert", "dp"), P("expert", None, "dp")),
        check_vma=False,
    )
```
